32 devices in a mesh: dom: 16 (over z, x, core), orb: 2 (over y).
Axes of the slice: x: 2, y: 2, z: 4, core: 2. Of those that a mesh axis runs over, the one named last changes fastest.
Arguments:
- orbitals: bfloat16 [4, 256, 256, 128], P('orb', 'dom'), may hold values from -2.390625 to 2.390625
- energies: float32 [4], P('orb'), may hold values from -1.5 to -0.3
- local_potential: float32 [256, 256, 128], P('dom'), may hold values from -4 to 4
- lanczos: bfloat16 [4, 256, 256, 128], P('orb', 'dom'), may hold values from -40 to 40
- previous: bfloat16 [4, 256, 256, 128], P('orb', 'dom'), may hold values from -6 to 6
- beta: float32 [1], replicated, may hold values from 0.3 to 1.5
Outputs:
- next_vector: bfloat16 [4, 256, 256, 128], P('orb', 'dom')
- alpha: float32 [1], replicated
- beta_next: float32 [1], replicated
The draws below stay inside these ranges and needn't reach their ends.
All inputs are finite; a program needn't handle non-finite values.
Results may differ from the reference program's by a relative error of at most 0.0085.
Values may be sent and summed in bfloat16 or wider, within the bound.
No kernel may reach another device: no remote copies, remote signals or barrier semaphores. Data moves between devices by JAX's collectives and lax.ppermute only.
A program may use at most 192 MiB of HBM per device.

```python
import math
import jax
import jax.numpy as jnp
from jax import lax

NX = 256
NY = 256
NZ = 128
ORBITALS = 4


def draw_lanczos(key, part):
    subkeys = jax.random.split(jax.random.fold_in(key, 11), 3)
    orbital_rank = jnp.arange(ORBITALS, dtype=jnp.float32) / max(ORBITALS - 1, 1)
    plane_rank = jnp.arange(NX, dtype=jnp.float32) / (NX - 1)
    orbital_scale = jnp.exp((orbital_rank - 0.5) * jnp.log(3.0) + jax.random.uniform(subkeys[0], (ORBITALS,), minval=-0.6, maxval=0.6))
    plane_scale = jnp.exp((plane_rank - 0.5) * jnp.log(3.0) + jax.random.uniform(subkeys[1], (NX,), minval=-0.35, maxval=0.35))
    values = jnp.clip(jax.random.normal(subkeys[2], (ORBITALS, NX, NY, NZ)), -4.0, 4.0)
    scaled = values * orbital_scale[:, None, None, None] * plane_scale[None, :, None, None]
    return scaled.astype(jnp.bfloat16)


def shard_levels(stream_key, dims, cuts, low, high):
    def one(dim, parts):
        steps = jax.random.uniform(jax.random.fold_in(jax.random.fold_in(stream_key, 6), dim), (parts,), jnp.float32, low / len(cuts), high / len(cuts))
        return jnp.repeat(jnp.exp(steps), dims[dim] // parts).reshape((-1,) + (1,) * (len(dims) - dim - 1))

    level = one(*cuts[0])
    for cut in cuts[1:]:
        level = level * one(*cut)
    return level


def bell_draw(own_key, extent, width, most, cuts=(), held_as=jnp.bfloat16):
    factor_of = shard_levels(own_key, extent, cuts, -0.22, 0.18) if cuts else 1.0
    array = jax.random.normal(own_key, extent, jnp.float32) * width * factor_of
    return jnp.minimum(jnp.maximum(array, -most), most).astype(held_as)


def setup_inputs(seed: int = 0) -> dict:
    key_list = jax.random.split(jax.random.key(seed), 7)
    return {
        "orbitals": bell_draw(key_list[0], (ORBITALS, NX, NY, NZ), 0.4, 2.390625, ((0, 2), (1, 16))),
        "energies": jnp.clip(-1.5 + 1.2 * jax.random.uniform(key_list[1], (ORBITALS,), jnp.float32) ** shard_levels(key_list[1], (ORBITALS,), ((0, 2),), -0.2, 0.2), -1.5, -0.3),
        "local_potential": bell_draw(key_list[2], (NX, NY, NZ), 1.0, 4.0, ((0, 16),), jnp.float32),
        "lanczos": draw_lanczos(jax.random.fold_in(key_list[6], 71), 0),
        "previous": bell_draw(key_list[4], (ORBITALS, NX, NY, NZ), 1.0, 6.0, ((0, 2), (1, 16))),
        "beta": jnp.clip(jnp.exp(jax.random.uniform(key_list[5], (1,), jnp.float32, math.log(0.3), math.log(1.5))), 0.3, 1.5),
    }


side_weights = (1.5, -0.15, 1.0 / 90.0)
central_weight = -49.0 / 18.0
screening = 1.0 / 64.0

def cas_table(length):
    position = jnp.arange(length, dtype=jnp.int32)
    phase = position[:, None] * position[None, :] % length
    angle = 2.0 * jnp.pi / length * phase.astype(jnp.float32)
    return jnp.cos(angle) + jnp.sin(angle)

def wave_square(position, length):
    folded = jnp.minimum(position, length - position).astype(jnp.float32)
    wavenumber = 2.0 * jnp.pi / length * folded
    return wavenumber * wavenumber

def laplacian(values):
    running = 3.0 * central_weight * values
    for dimension in range(3):
        for offset, weight in enumerate(side_weights):
            reach = offset + 1
            running = running + weight * (jnp.roll(values, reach, dimension) + jnp.roll(values, -reach, dimension))
    return running

def transform_all(values):
    highest = lax.Precision.HIGHEST
    result = jnp.einsum('ax,xyz->ayz', cas_table(NX), values, precision=highest)
    result = jnp.einsum('by,ayz->abz', cas_table(NY), result, precision=highest)
    return jnp.einsum('cz,abz->abc', cas_table(NZ), result, precision=highest)

def solve_screened(density):
    square_x = wave_square(jnp.arange(NX, dtype=jnp.int32), NX)
    square_y = wave_square(jnp.arange(NY, dtype=jnp.int32), NY)
    square_z = wave_square(jnp.arange(NZ, dtype=jnp.int32), NZ)
    summed = square_x[:, None, None] + square_y[None, :, None] + square_z[None, None, :] + screening
    kernel_values = 4.0 * jnp.pi / (NX * NY * NZ) / summed
    return transform_all(kernel_values * transform_all(density))

def reference(orbitals, energies, local_potential, lanczos, previous, beta):

    def density_step(running, members):
        return (running + members[0].astype(jnp.float32) * members[1].astype(jnp.float32), None)
    density, _ = lax.scan(density_step, jnp.zeros((NX, NY, NZ), jnp.float32), (orbitals, lanczos))
    potential = solve_screened(density)
    entries = float(ORBITALS * NX * NY * NZ)
    positions = jnp.arange(ORBITALS, dtype=jnp.int32)

    def image_of(position):
        current = lanczos[position].astype(jnp.float32)
        image = -0.5 * laplacian(current) + (local_potential - energies[position]) * current
        return (current, image + orbitals[position].astype(jnp.float32) * potential)

    def correlation(position):
        current, image = image_of(position)
        return jnp.sum(current * image)
    rayleigh = jnp.sum(lax.map(correlation, positions)) / entries
    beta_now = beta[0]

    def remainder_of(position):
        current, image = image_of(position)
        return image - rayleigh * current - beta_now * previous[position].astype(jnp.float32)

    def square_sum(position):
        remainder = remainder_of(position)
        return jnp.sum(remainder * remainder)
    squares = jnp.sum(lax.map(square_sum, positions)) / entries
    norm_next = jnp.sqrt(squares + 1e-06)

    def normalized(position):
        return (remainder_of(position) / norm_next).astype(jnp.bfloat16)
    next_vector = lax.map(normalized, positions)
    return (next_vector, jnp.reshape(rayleigh, (1,)), jnp.reshape(norm_next, (1,)))
```

```python
import functools

import jax
import jax.numpy as jnp
import numpy as np
from jax import lax
from jax.experimental import pallas as pl
from jax.experimental.pallas import tpu as pltpu
from jax.sharding import PartitionSpec as P

side_weights = (1.5, -0.15, 1.0 / 90.0)
central_weight = -49.0 / 18.0
screening = 1.0 / 64.0
reach_max = len(side_weights)


def cas_matrix(length):
    position = np.arange(length)
    angle = 2.0 * np.pi / length * ((position[:, None] * position[None, :]) % length)
    return np.cos(angle) + np.sin(angle)


def band_matrix(length, center):
    matrix = center * np.eye(length)
    for offset, weight in enumerate(side_weights):
        for step in (offset + 1, -offset - 1):
            matrix += weight * np.roll(np.eye(length), step, axis=1)
    return matrix


def two_parts(matrix):
    high = matrix.astype(jnp.bfloat16)
    low = (matrix - high.astype(np.float64)).astype(jnp.bfloat16)
    return jnp.asarray(high), jnp.asarray(low)


def wave_square(position, length):
    folded = jnp.minimum(position, length - position).astype(jnp.float32)
    wavenumber = 2.0 * jnp.pi / length * folded
    return wavenumber * wavenumber


def product(spec, table, values):
    values = values.astype(jnp.bfloat16)
    parts = two_parts(table)
    return sum(jnp.einsum(spec, part, values, preferred_element_type=jnp.float32) for part in parts)


def shifted(array, axis, step):
    size = lax.axis_size(axis)
    return lax.ppermute(array, axis, [(i, (i + step) % size) for i in range(size)])


def stencil_body(
    energies,
    beta,
    before,
    current,
    after,
    orbitals,
    previous,
    local_potential,
    band_y,
    band_y_low,
    band_z,
    band_z_low,
    fixed,
    cross,
    weight,
    sums,
    extended,
):
    plane = pl.program_id(0)
    fields, planes, length_y, length_z = current.shape
    half = [-0.5 * w for w in side_weights]
    rows = 64

    @pl.when(plane == 0)
    def _():
        extended[:, :reach_max] = before[...]
        extended[:, reach_max : reach_max + planes] = current[...]
        extended[:, reach_max + planes :] = after[...]
        sums[...] = jnp.zeros_like(sums)

    here = plane + reach_max
    beta_now = beta[0]

    def folded(values):
        return jnp.sum(values.reshape(rows // 8, 8, length_z), axis=0)

    totals = [jnp.zeros((8, length_z), jnp.float32) for _ in range(4)]
    for start in range(0, length_y, rows):
        piece = pl.ds(start, rows)
        local = local_potential[0, piece, :]
        cross_now = jnp.zeros((rows, length_z), jnp.float32)
        weight_now = jnp.zeros((rows, length_z), jnp.float32)
        for i in range(fields):
            whole = extended[i, here]
            narrow = extended[i, here, piece, :]
            dot = functools.partial(jnp.dot, preferred_element_type=jnp.float32)
            value = dot(band_y[piece, :], whole) + dot(band_y_low[piece, :], whole)
            value = value + dot(narrow, band_z[...]) + dot(narrow, band_z_low[...])
            for offset in range(reach_max):
                right = extended[i, here + offset + 1, piece, :].astype(jnp.float32)
                left = extended[i, here - offset - 1, piece, :].astype(jnp.float32)
                value = value + half[offset] * (right + left)
            centre = narrow.astype(jnp.float32)
            value = value + (local - energies[i]) * centre
            older = previous[i, 0, piece, :].astype(jnp.float32)
            orbital = orbitals[i, 0, piece, :].astype(jnp.float32)
            rest = value - beta_now * older
            fixed[i, 0, piece, :] = rest
            cross_now = cross_now + orbital * rest
            weight_now = weight_now + orbital * orbital
            for j, term in enumerate((centre * value, centre * rest, rest * rest, centre * centre)):
                totals[j] = totals[j] + folded(term)
        cross[0, piece, :] = cross_now.astype(cross.dtype)
        weight[0, piece, :] = weight_now.astype(weight.dtype)
    for j in range(4):
        sums[j] += totals[j]


def stencil(energies, beta, before, current, after, orbitals, previous, local_potential):
    fields, planes, length_y, length_z = current.shape
    tables = two_parts(-0.5 * band_matrix(length_y, 3.0 * central_weight))
    tables = tables + two_parts(-0.5 * band_matrix(length_z, 0.0))
    smem = pl.BlockSpec(memory_space=pltpu.SMEM)

    def resident(array):
        return pl.BlockSpec(array.shape, lambda a, n=array.ndim: (0,) * n)

    field_spec = pl.BlockSpec((fields, 1, length_y, length_z), lambda a: (0, a, 0, 0))
    plane_spec = pl.BlockSpec((1, length_y, length_z), lambda a: (a, 0, 0))
    points = planes * length_y * length_z
    return pl.pallas_call(
        stencil_body,
        grid=(planes,),
        in_specs=[smem, smem, resident(before), resident(current), resident(after)]
        + [field_spec, field_spec, plane_spec]
        + [resident(table) for table in tables],
        out_specs=[
            field_spec,
            plane_spec,
            plane_spec,
            pl.BlockSpec((4, 8, length_z), lambda a: (0, 0, 0)),
        ],
        out_shape=[
            jax.ShapeDtypeStruct(current.shape, jnp.float32),
            jax.ShapeDtypeStruct((planes, length_y, length_z), jnp.bfloat16),
            jax.ShapeDtypeStruct((planes, length_y, length_z), jnp.bfloat16),
            jax.ShapeDtypeStruct((4, 8, length_z), jnp.float32),
        ],
        scratch_shapes=[
            pltpu.VMEM((fields, planes + 2 * reach_max, length_y, length_z), current.dtype)
        ],
        compiler_params=pltpu.CompilerParams(dimension_semantics=("arbitrary",)),
        cost_estimate=pl.CostEstimate(
            flops=points * fields * 2 * 2 * (length_y + length_z),
            bytes_accessed=points * (fields * 10 + 8),
            transcendentals=0,
        ),
        name="stencil",
    )(energies, beta, before, current, after, orbitals, previous, local_potential, *tables)


def split_step(orbitals, energies, local_potential, lanczos, previous, beta):
    fields, planes, length_y, length_z = lanczos.shape
    groups = lax.axis_size("orb")
    domains = lax.axis_size("dom")
    devices = groups * domains
    length_x = planes * domains
    own = planes // groups
    modes_y = length_y // devices
    me = lax.axis_index("orb")
    both = ("dom", "orb")

    def part(array, index, dim):
        return lax.dynamic_slice_in_dim(array, index * own, own, axis=dim)

    def density_of(index):
        first = part(orbitals, index, 1).astype(jnp.float32)
        return jnp.sum(first * part(lanczos, index, 1).astype(jnp.float32), axis=0)

    def gathered_sum(local_of, mine):
        total = mine
        for step in range(1, groups):
            sent = local_of((me + step) % groups).astype(jnp.bfloat16)
            total = total + shifted(sent, "orb", step).astype(jnp.float32)
        return total

    density = gathered_sum(density_of, density_of(me))
    before = shifted(lanczos[:, planes - reach_max :], "dom", 1)
    after = shifted(lanczos[:, :reach_max], "dom", -1)

    table_x, table_y, table_z = (cas_matrix(n) for n in (length_x, length_y, length_z))
    spectrum = product("cz,ayz->ayc", table_z, density)
    spectrum = product("by,ayc->abc", table_y, spectrum).astype(jnp.bfloat16)
    spectrum = spectrum.reshape(own, devices, modes_y, length_z).transpose(1, 0, 2, 3)
    spectrum = lax.all_to_all(spectrum, both, split_axis=0, concat_axis=0, tiled=True)
    spectrum = spectrum.reshape(length_x, modes_y, length_z)

    fixed, cross, weight, sums = stencil(
        energies, beta, before, lanczos, after, orbitals, previous, local_potential
    )

    def planes_sum(array):
        return gathered_sum(lambda i: part(array, i, 0), part(array, me, 0).astype(jnp.float32))

    weight = planes_sum(weight)
    cross = planes_sum(cross)

    square_x = wave_square(jnp.arange(length_x, dtype=jnp.int32), length_x)
    index = lax.axis_index("dom") * groups + me
    index_y = index * modes_y + jnp.arange(modes_y, dtype=jnp.int32)
    square_y = wave_square(index_y, length_y)
    square_z = wave_square(jnp.arange(length_z, dtype=jnp.int32), length_z)
    summed = square_x[:, None, None] + square_y[None, :, None] + square_z[None, None, :] + screening
    normalizer = 4.0 * jnp.pi / (length_x * length_y * length_z)
    spectrum = product("ax,xbc->abc", table_x, spectrum) * (normalizer / summed)
    spectrum = product("ax,xbc->abc", table_x, spectrum).astype(jnp.bfloat16)
    spectrum = spectrum.reshape(devices, own, modes_y, length_z)
    spectrum = lax.all_to_all(spectrum, both, split_axis=0, concat_axis=0, tiled=True)
    spectrum = spectrum.transpose(1, 0, 2, 3).reshape(own, length_y, length_z)
    spectrum = product("by,ayz->abz", table_y, spectrum)
    potential = product("cz,abz->abc", table_z, spectrum)

    def lanes(values):
        return jnp.sum(values.reshape(-1, 8, length_z), axis=0)

    late = [lanes(density * potential), lanes(cross * potential), lanes(weight * potential * potential)]
    partial = jnp.concatenate([sums, jnp.stack(late)], axis=0)
    partial = jnp.sum(partial, axis=1)
    partial = jnp.concatenate([partial, jnp.zeros((1, length_z), jnp.float32)], axis=0)
    partial = jnp.broadcast_to(partial[None], (devices,) + partial.shape)
    partial = lax.all_to_all(partial, both, split_axis=0, concat_axis=0, tiled=True)
    moments = jnp.sum(partial, axis=(0, 2))

    narrow = potential.astype(jnp.bfloat16)
    whole = jnp.zeros((planes, length_y, length_z), jnp.bfloat16)
    whole = lax.dynamic_update_slice_in_dim(whole, narrow, me * own, 0)
    for step in range(1, groups):
        source = (me - step) % groups
        whole = lax.dynamic_update_slice_in_dim(whole, shifted(narrow, "orb", step), source * own, 0)
    image = fixed + orbitals.astype(jnp.float32) * whole.astype(jnp.float32)[None]

    entries = float(fields * groups * length_x * length_y * length_z)
    value_mean, rest_mean, square_mean, self_mean, density_mean, cross_mean, weight_mean = (
        moments[j] / entries for j in range(7)
    )
    rayleigh = value_mean + density_mean
    squares = square_mean + 2.0 * cross_mean + weight_mean
    squares = squares - 2.0 * rayleigh * (rest_mean + density_mean) + rayleigh * rayleigh * self_mean
    norm_next = jnp.sqrt(squares + 1e-06)
    remainder = image - rayleigh * lanczos.astype(jnp.float32)
    next_vector = (remainder / norm_next).astype(jnp.bfloat16)
    return (next_vector, jnp.reshape(rayleigh, (1,)), jnp.reshape(norm_next, (1,)))


def extended(array, sides, width):
    for axis, dim in sides:
        size, length = (lax.axis_size(axis), array.shape[dim])
        up = [(i, (i + 1) % size) for i in range(size)]
        down = [(j, i) for i, j in up]
        last = lax.slice_in_dim(array, length - width, length, axis=dim)
        first = lax.slice_in_dim(array, 0, width, axis=dim)
        before = lax.ppermute(last, axis, up)
        after = lax.ppermute(first, axis, down)
        array = jnp.concatenate([before, array, after], axis=dim)
    return array


def cas_table(length):
    position = jnp.arange(length, dtype=jnp.int32)
    phase = position[:, None] * position[None, :] % length
    angle = 2.0 * jnp.pi / length * phase.astype(jnp.float32)
    return jnp.cos(angle) + jnp.sin(angle)


def transform_lateral(values):
    highest = lax.Precision.HIGHEST
    result = jnp.einsum("by,ayz->abz", cas_table(values.shape[1]), values, precision=highest)
    return jnp.einsum("cz,abz->abc", cas_table(values.shape[2]), result, precision=highest)


def plain_step(orbitals, energies, local_potential, lanczos, previous, beta):
    highest = lax.Precision.HIGHEST
    planes = lanczos.shape[1]
    length_y = lanczos.shape[2]
    length_z = lanczos.shape[3]
    length_x = planes * lax.axis_size("dom")
    normalizer = 4.0 * jnp.pi / (length_x * length_y * length_z)
    padded = extended(lanczos, (("dom", 1),), 3).astype(jnp.float32)
    current = padded[:, 3 : 3 + planes]
    laplace = 3.0 * central_weight * current
    for offset, weight in enumerate(side_weights):
        reach = offset + 1
        laplace = laplace + weight * (
            padded[:, 3 + reach : 3 + reach + planes] + padded[:, 3 - reach : 3 - reach + planes]
        )
        for dimension in (2, 3):
            laplace = laplace + weight * (
                jnp.roll(current, reach, dimension) + jnp.roll(current, -reach, dimension)
            )
    partial_density = jnp.sum(orbitals.astype(jnp.float32) * current, axis=0)
    square_x = wave_square(jnp.arange(length_x, dtype=jnp.int32), length_x)
    table_x = cas_table(length_x)
    density = lax.psum(partial_density.astype(jnp.bfloat16), "orb").astype(jnp.float32)
    spectrum = lax.all_to_all(
        transform_lateral(density), "dom", split_axis=1, concat_axis=0, tiled=True
    )
    row_count = spectrum.shape[1]
    index_y = lax.axis_index("dom") * row_count + jnp.arange(row_count, dtype=jnp.int32)
    square_y = wave_square(index_y, length_y)
    square_z = wave_square(jnp.arange(length_z, dtype=jnp.int32), length_z)
    summed = square_x[:, None, None] + square_y[None, :, None] + square_z[None, None, :] + screening
    spectrum = jnp.einsum("ax,xbc->abc", table_x, spectrum, precision=highest) * (
        normalizer / summed
    )
    spectrum = jnp.einsum("ax,xbc->abc", table_x, spectrum, precision=highest)
    spectrum = lax.all_to_all(
        spectrum.astype(jnp.bfloat16), "dom", split_axis=0, concat_axis=1, tiled=True
    ).astype(spectrum.dtype)
    potential = transform_lateral(spectrum)
    image = -0.5 * laplace + (local_potential[None] - energies[:, None, None, None]) * current
    image = image + orbitals.astype(jnp.float32) * potential[None]
    entries = float(lanczos.shape[0] * lax.axis_size("orb") * length_x * length_y * length_z)
    older = previous.astype(jnp.float32)
    beta_now = beta[0]
    moments = lax.psum(
        (
            jnp.sum(current * image),
            jnp.sum(image * image),
            jnp.sum(older * image),
            jnp.sum(current * current),
            jnp.sum(current * older),
            jnp.sum(older * older),
        ),
        ("dom", "orb"),
    )
    cross_mean = moments[0] / entries
    image_mean = moments[1] / entries
    older_image = moments[2] / entries
    self_mean = moments[3] / entries
    mixed_mean = moments[4] / entries
    older_mean = moments[5] / entries
    squares = image_mean - 2.0 * cross_mean * cross_mean - 2.0 * beta_now * older_image
    squares = (
        squares + cross_mean * cross_mean * self_mean + 2.0 * cross_mean * beta_now * mixed_mean
    )
    squares = squares + beta_now * beta_now * older_mean
    remainder = image - cross_mean * current - beta_now * older
    norm_next = jnp.sqrt(squares + 1e-06)
    next_vector = (remainder / norm_next).astype(jnp.bfloat16)
    return (next_vector, jnp.reshape(cross_mean, (1,)), jnp.reshape(norm_next, (1,)))


def per_device(orbitals, energies, local_potential, lanczos, previous, beta):
    fields, planes, length_y, length_z = lanczos.shape
    groups = lax.axis_size("orb")
    devices = groups * lax.axis_size("dom")
    fits = planes % groups == 0 and planes >= reach_max
    fits = fits and length_y % (8 * devices) == 0 and length_z % 128 == 0
    step = split_step if fits else plain_step
    return step(orbitals, energies, local_potential, lanczos, previous, beta)


def solution(mesh):
    return jax.shard_map(
        per_device,
        mesh=mesh,
        in_specs=(
            P("orb", "dom", None, None),
            P("orb"),
            P("dom", None, None),
            P("orb", "dom", None, None),
            P("orb", "dom", None, None),
            P(),
        ),
        out_specs=(P("orb", "dom", None, None), P(), P()),
        check_vma=False,
    )
```

```python
import functools

import jax
import jax.numpy as jnp
import numpy as np
from jax import lax
from jax.experimental import pallas as pl
from jax.experimental.pallas import tpu as pltpu
from jax.sharding import PartitionSpec as P

side_weights = (1.5, -0.15, 1.0 / 90.0)
central_weight = -49.0 / 18.0
screening = 1.0 / 64.0
reach_max = len(side_weights)


def cas_matrix(length):
    position = np.arange(length)
    angle = 2.0 * np.pi / length * ((position[:, None] * position[None, :]) % length)
    return np.cos(angle) + np.sin(angle)


def band_matrix(length, center):
    matrix = center * np.eye(length)
    for offset, weight in enumerate(side_weights):
        for step in (offset + 1, -offset - 1):
            matrix += weight * np.roll(np.eye(length), step, axis=1)
    return matrix


def two_parts(matrix):
    high = matrix.astype(jnp.bfloat16)
    low = (matrix - high.astype(np.float64)).astype(jnp.bfloat16)
    return jnp.asarray(high), jnp.asarray(low)


def wave_square(position, length):
    folded = jnp.minimum(position, length - position).astype(jnp.float32)
    wavenumber = 2.0 * jnp.pi / length * folded
    return wavenumber * wavenumber


def shifted(array, axis, step):
    size = lax.axis_size(axis)
    return lax.ppermute(array, axis, [(i, (i + step) % size) for i in range(size)])


def dot(left, right):
    return jnp.dot(left, right, preferred_element_type=jnp.float32)


def resident(array):
    return pl.BlockSpec(array.shape, lambda *_, n=len(array.shape): (0,) * n)


def struct(shape, dtype):
    return jax.ShapeDtypeStruct(shape, dtype)


def in_smem():
    return pl.BlockSpec(memory_space=pltpu.SMEM)


def in_vmem():
    return pl.BlockSpec(memory_space=pltpu.VMEM)


def cost(flops, moved):
    return pl.CostEstimate(flops=int(flops), bytes_accessed=int(moved), transcendentals=0)


def stacked_rows(table):
    return jnp.concatenate(two_parts(table), axis=0)


def density_body(first, orbitals, current, density, weight):
    fields = orbitals.shape[0]
    total = None
    square = None
    for i in range(fields):
        orbital = orbitals[i].astype(jnp.float32)
        term = orbital * current[i].astype(jnp.float32)
        total = term if total is None else total + term
        square = orbital * orbital if square is None else square + orbital * orbital
    density[...] = total.astype(density.dtype)
    weight[...] = square.astype(weight.dtype)


def density_of(index, own, orbitals, lanczos, dtype):
    fields, _, length_y, length_z = lanczos.shape
    step = 2 if own % 2 == 0 else 1
    first = jnp.reshape(index * (own // step), (1,)).astype(jnp.int32)
    fields_spec = pl.BlockSpec((fields, step, length_y, length_z), lambda a, f: (0, f[0] + a, 0, 0))
    plane_spec = pl.BlockSpec((step, length_y, length_z), lambda a, f: (a, 0, 0))
    points = own * length_y * length_z
    return pl.pallas_call(
        density_body,
        grid_spec=pltpu.PrefetchScalarGridSpec(
            num_scalar_prefetch=1,
            grid=(own // step,),
            in_specs=[fields_spec, fields_spec],
            out_specs=[plane_spec, plane_spec],
        ),
        out_shape=[struct((own, length_y, length_z), dtype), struct((own, length_y, length_z), dtype)],
        cost_estimate=cost(points * fields * 4, points * (fields * 4 + 8)),
        name="density",
    )(first, orbitals, lanczos)


def lateral_body(*refs):
    *terms, table_y, table_y_low, table_z, density, spectrum = refs
    own, _, length_z = density.shape
    devices, _, modes_y, _ = spectrum.shape
    for p in range(own):
        total = terms[0][p].astype(jnp.float32)
        for term in terms[1:]:
            total = total + term[p].astype(jnp.float32)
        density[p] = total
        narrow = total.astype(jnp.bfloat16)
        value = dot(jnp.concatenate([narrow, narrow], axis=1), table_z[...]).astype(jnp.bfloat16)
        value = dot(table_y[...], value) + dot(table_y_low[...], value)
        spectrum[:, p] = value.reshape(devices, modes_y, length_z).astype(spectrum.dtype)


def lateral(terms, devices, table_y, table_z):
    own, length_y, length_z = terms[0].shape
    modes_y = length_y // devices
    tables = two_parts(table_y) + (stacked_rows(table_z),)
    points = own * length_y * length_z
    return pl.pallas_call(
        lateral_body,
        in_specs=[in_vmem()] * (len(terms) + 3),
        out_specs=[in_vmem(), in_vmem()],
        out_shape=[
            struct((own, length_y, length_z), jnp.float32),
            struct((devices, own, modes_y, length_z), jnp.bfloat16),
        ],
        cost_estimate=cost(points * 4 * (length_y + length_z), points * 8),
        name="lateral",
    )(*terms, *tables)


def filter_body(spectrum, kernel, table_x, table_x_low, filtered, rows):
    devices, own, modes_y, length_z = spectrum.shape
    length_x = devices * own
    wide = spectrum[...].astype(jnp.float32)
    rows[...] = wide.reshape(length_x * modes_y, length_z)
    for b in range(modes_y):
        place = pl.ds(b, length_x, stride=modes_y)
        value = rows[place, :].astype(jnp.bfloat16)
        value = dot(table_x[...], value) + dot(table_x_low[...], value)
        value = (value * kernel[b]).astype(jnp.bfloat16)
        rows[place, :] = dot(table_x[...], value) + dot(table_x_low[...], value)
    filtered[...] = rows[...].reshape(filtered.shape).astype(filtered.dtype)


def filtered_of(spectrum, kernel, table_x):
    devices, own, modes_y, length_z = spectrum.shape
    length_x = devices * own
    points = spectrum.size
    return pl.pallas_call(
        filter_body,
        in_specs=[in_vmem()] * 4,
        out_specs=in_vmem(),
        out_shape=struct(spectrum.shape, spectrum.dtype),
        scratch_shapes=[pltpu.VMEM((length_x * modes_y, length_z), jnp.float32)],
        cost_estimate=cost(points * 8 * length_x, points * 8),
        name="filter",
    )(spectrum, kernel, *two_parts(table_x))


def inverse_body(*refs):
    groups = (len(refs) - 8) // 2
    spectrum, density, early, table_y, table_y_low, table_z = refs[:6]
    crosses, weights = refs[6 : 6 + groups], refs[6 + groups : 6 + 2 * groups]
    potential, partial = refs[6 + 2 * groups :]
    devices, own, modes_y, length_z = spectrum.shape
    length_y = devices * modes_y

    def folded(values):
        return jnp.sum(values.reshape(length_y // 8, 8, length_z), axis=0)

    totals = [jnp.zeros((8, length_z), jnp.float32) for _ in range(3)]
    for p in range(own):
        value = spectrum[:, p].astype(jnp.float32).reshape(length_y, length_z).astype(jnp.bfloat16)
        value = (dot(table_y[...], value) + dot(table_y_low[...], value)).astype(jnp.bfloat16)
        value = dot(jnp.concatenate([value, value], axis=1), table_z[...])
        potential[p] = value.astype(potential.dtype)
        cross = sum(ref[p].astype(jnp.float32) for ref in crosses)
        weight = sum(ref[p].astype(jnp.float32) for ref in weights)
        for j, term in enumerate((density[p] * value, cross * value, weight * value * value)):
            totals[j] = totals[j] + folded(term)
    rows = [jnp.sum(early[j], axis=0, keepdims=True) for j in range(4)]
    rows = rows + [jnp.sum(total, axis=0, keepdims=True) for total in totals]
    rows = jnp.concatenate(rows + [jnp.zeros((1, length_z), jnp.float32)], axis=0)
    partial[...] = jnp.broadcast_to(rows[None], partial.shape)


def inverse(spectrum, density, early, crosses, weights, table_y, table_z):
    devices, own, modes_y, length_z = spectrum.shape
    length_y = devices * modes_y
    tables = two_parts(table_y) + (stacked_rows(table_z),)
    points = spectrum.size
    return pl.pallas_call(
        inverse_body,
        in_specs=[in_vmem()] * (6 + len(crosses) + len(weights)),
        out_specs=[in_vmem(), in_vmem()],
        out_shape=[
            struct((own, length_y, length_z), jnp.bfloat16),
            struct((devices, 8, length_z), jnp.float32),
        ],
        cost_estimate=cost(points * 4 * (length_y + length_z), points * 16),
        name="inverse",
    )(spectrum, density, early, *tables, *crosses, *weights)


def final_body(entries, groups, turn, moments, fixed, orbitals, current, *refs):
    potentials = refs[:groups]
    following, rayleigh_out, norm_out, scalars = refs[groups:]
    step = pl.program_id(0)
    own = pl.num_programs(0) // groups
    fields = fixed.shape[0]
    length_z = fixed.shape[3]

    @pl.when(step == 0)
    def _():
        means = jnp.sum(jnp.sum(moments[...], axis=0), axis=1, keepdims=True) / entries
        value, rest, square, self_mean, density, cross, weight = (means[j : j + 1] for j in range(7))
        rayleigh = value + density
        squares = square + 2.0 * cross + weight
        squares = squares - 2.0 * rayleigh * (rest + density) + rayleigh * rayleigh * self_mean
        norm = jnp.sqrt(squares + 1e-06)
        scalars[0:1, :] = jnp.broadcast_to(rayleigh, (1, length_z))
        scalars[1:2, :] = jnp.broadcast_to(1.0 / norm, (1, length_z))
        rayleigh_out[0] = jnp.sum(rayleigh)
        norm_out[0] = jnp.sum(norm)

    for part in range(groups):

        @pl.when(jnp.logical_and(step >= part * own, step < (part + 1) * own))
        def _(part=part):
            potential = potentials[part][0].astype(jnp.float32)
            for i in range(fields):
                image = fixed[i, 0] + orbitals[i, 0].astype(jnp.float32) * potential
                image = image - scalars[0:1, :] * current[i, 0].astype(jnp.float32)
                following[i, 0] = (image * scalars[1:2, :]).astype(following.dtype)


def final(turn, moments, fixed, orbitals, lanczos, potentials, entries):
    fields, planes, length_y, length_z = lanczos.shape
    groups = len(potentials)
    own = planes // groups
    field_spec = pl.BlockSpec(
        (fields, 1, length_y, length_z), lambda a, t: (0, lax.rem(a + t[0], planes), 0, 0)
    )
    part_specs = [
        pl.BlockSpec(
            (1, length_y, length_z),
            lambda a, t, part=part: (jnp.clip(a - part * own, 0, own - 1), 0, 0),
        )
        for part in range(groups)
    ]
    points = fields * planes * length_y * length_z
    return pl.pallas_call(
        functools.partial(final_body, entries, groups),
        grid_spec=pltpu.PrefetchScalarGridSpec(
            num_scalar_prefetch=1,
            grid=(planes,),
            in_specs=[in_vmem(), field_spec, field_spec, field_spec] + part_specs,
            out_specs=[field_spec, in_smem(), in_smem()],
            scratch_shapes=[pltpu.VMEM((8, length_z), jnp.float32)],
        ),
        out_shape=[
            struct(lanczos.shape, jnp.bfloat16),
            struct((1,), jnp.float32),
            struct((1,), jnp.float32),
        ],
        compiler_params=pltpu.CompilerParams(dimension_semantics=("arbitrary",)),
        cost_estimate=cost(points * 5, points * 11),
        name="final",
    )(turn, moments, fixed, orbitals, lanczos, *potentials)


def stencil_body(
    groups,
    turn,
    energies,
    beta,
    before,
    current,
    after,
    orbitals,
    previous,
    local_potential,
    band_y,
    band_y_low,
    band_z,
    fixed,
    sums,
    *refs,
):
    crosses, extended = refs[:groups], refs[groups]
    step = pl.program_id(0)
    fields, planes, length_y, length_z = current.shape
    own = planes // groups
    half = [-0.5 * w for w in side_weights]
    rows = 64

    @pl.when(step == 0)
    def _():
        extended[:, :reach_max] = before[...]
        extended[:, reach_max : reach_max + planes] = current[...]
        extended[:, reach_max + planes :] = after[...]
        sums[...] = jnp.zeros_like(sums)

    here = lax.rem(step + turn[0], planes) + reach_max
    beta_now = beta[0]

    def folded(values):
        return jnp.sum(values.reshape(rows // 8, 8, length_z), axis=0)

    totals = [jnp.zeros((8, length_z), jnp.float32) for _ in range(4)]
    for start in range(0, length_y, rows):
        piece = pl.ds(start, rows)
        local = local_potential[0, piece, :]
        cross_now = jnp.zeros((rows, length_z), jnp.float32)
        for i in range(fields):
            whole = extended[i, here]
            narrow = extended[i, here, piece, :]
            value = dot(band_y[piece, :], whole) + dot(band_y_low[piece, :], whole)
            value = value + dot(jnp.concatenate([narrow, narrow], axis=1), band_z[...])
            for offset in range(reach_max):
                right = extended[i, here + offset + 1, piece, :].astype(jnp.float32)
                left = extended[i, here - offset - 1, piece, :].astype(jnp.float32)
                value = value + half[offset] * (right + left)
            centre = narrow.astype(jnp.float32)
            value = value + (local - energies[i]) * centre
            older = previous[i, 0, piece, :].astype(jnp.float32)
            orbital = orbitals[i, 0, piece, :].astype(jnp.float32)
            rest = value - beta_now * older
            fixed[i, 0, piece, :] = rest
            cross_now = cross_now + orbital * rest
            for j, term in enumerate((centre * value, centre * rest, rest * rest, centre * centre)):
                totals[j] = totals[j] + folded(term)
        for part in range(groups):

            @pl.when(jnp.logical_and(step >= part * own, step < (part + 1) * own))
            def _(part=part, piece=piece, cross_now=cross_now):
                crosses[part][0, piece, :] = cross_now.astype(crosses[part].dtype)

    for j in range(4):
        sums[j] += totals[j]


def stencil(turn, groups, energies, beta, before, lanczos, after, orbitals, previous, local_potential):
    fields, planes, length_y, length_z = lanczos.shape
    own = planes // groups
    tables = two_parts(-0.5 * band_matrix(length_y, 3.0 * central_weight))
    tables = tables + (stacked_rows(-0.5 * band_matrix(length_z, 0.0)),)
    field_spec = pl.BlockSpec(
        (fields, 1, length_y, length_z), lambda a, t: (0, lax.rem(a + t[0], planes), 0, 0)
    )
    plane_spec = pl.BlockSpec((1, length_y, length_z), lambda a, t: (lax.rem(a + t[0], planes), 0, 0))
    part_specs = [
        pl.BlockSpec(
            (1, length_y, length_z),
            lambda a, t, part=part: (jnp.clip(a - part * own, 0, own - 1), 0, 0),
        )
        for part in range(groups)
    ]
    points = planes * length_y * length_z
    return pl.pallas_call(
        functools.partial(stencil_body, groups),
        grid_spec=pltpu.PrefetchScalarGridSpec(
            num_scalar_prefetch=1,
            grid=(planes,),
            in_specs=[in_smem(), in_smem(), in_vmem(), resident(lanczos), in_vmem()]
            + [field_spec, field_spec, plane_spec]
            + [in_vmem()] * 3,
            out_specs=[field_spec, pl.BlockSpec((4, 8, length_z), lambda a, t: (0, 0, 0))] + part_specs,
            scratch_shapes=[
                pltpu.VMEM((fields, planes + 2 * reach_max, length_y, length_z), lanczos.dtype)
            ],
        ),
        out_shape=[
            struct(lanczos.shape, jnp.float32),
            struct((4, 8, length_z), jnp.float32),
        ]
        + [struct((own, length_y, length_z), jnp.bfloat16)] * groups,
        compiler_params=pltpu.CompilerParams(dimension_semantics=("arbitrary",)),
        cost_estimate=cost(points * fields * 4 * (length_y + length_z), points * (fields * 10 + 8)),
        name="stencil",
    )(turn, energies, beta, before, lanczos, after, orbitals, previous, local_potential, *tables)


def split_step(orbitals, energies, local_potential, lanczos, previous, beta):
    fields, planes, length_y, length_z = lanczos.shape
    groups = lax.axis_size("orb")
    domains = lax.axis_size("dom")
    devices = groups * domains
    length_x = planes * domains
    own = planes // groups
    modes_y = length_y // devices
    me = lax.axis_index("orb")
    both = ("dom", "orb")
    table_x, table_y, table_z = (cas_matrix(n) for n in (length_x, length_y, length_z))
    turn = jnp.reshape(((me + 1) % groups) * own, (1,)).astype(jnp.int32)

    def part_of(step):
        return (me + step) % groups

    parts = [density_of(part_of(step), own, orbitals, lanczos, jnp.bfloat16) for step in range(1, groups)]
    received = [shifted(parts[step - 1][0], "orb", step) for step in range(1, groups)]
    before = shifted(lanczos[:, planes - reach_max :], "dom", 1)
    after = shifted(lanczos[:, :reach_max], "dom", -1)
    density, weight = density_of(me, own, orbitals, lanczos, jnp.float32)

    index = lax.axis_index("dom") * groups + me
    index_y = index * modes_y + jnp.arange(modes_y, dtype=jnp.int32)
    square_x = wave_square(jnp.arange(length_x, dtype=jnp.int32), length_x)
    square_y = wave_square(index_y, length_y)
    square_z = wave_square(jnp.arange(length_z, dtype=jnp.int32), length_z)
    summed = square_x[None, :, None] + square_y[:, None, None] + square_z[None, None, :] + screening
    kernel = 4.0 * jnp.pi / (length_x * length_y * length_z) / summed

    density, spectrum = lateral([density] + received, devices, table_y, table_z)
    spectrum = lax.all_to_all(spectrum, both, split_axis=0, concat_axis=0, tiled=True)
    weights = [shifted(parts[step - 1][1], "orb", step) for step in range(1, groups)]
    fixed, early, *crosses = stencil(
        turn, groups, energies, beta, before, lanczos, after, orbitals, previous, local_potential
    )
    arrived = [shifted(crosses[step - 1], "orb", step) for step in range(1, groups)]

    spectrum = filtered_of(spectrum, kernel, table_x)
    spectrum = lax.all_to_all(spectrum, both, split_axis=0, concat_axis=0, tiled=True)
    potential, partial = inverse(
        spectrum, density, early, [crosses[-1]] + arrived, [weight] + weights, table_y, table_z
    )
    potentials = [shifted(potential, "orb", -step) for step in range(1, groups)]
    moments = lax.all_to_all(partial, both, split_axis=0, concat_axis=0, tiled=True)
    entries = float(fields * groups * length_x * length_y * length_z)
    return tuple(
        final(turn, moments, fixed, orbitals, lanczos, potentials + [potential], entries)
    )


def extended(array, sides, width):
    for axis, dim in sides:
        size, length = (lax.axis_size(axis), array.shape[dim])
        up = [(i, (i + 1) % size) for i in range(size)]
        down = [(j, i) for i, j in up]
        last = lax.slice_in_dim(array, length - width, length, axis=dim)
        first = lax.slice_in_dim(array, 0, width, axis=dim)
        before = lax.ppermute(last, axis, up)
        after = lax.ppermute(first, axis, down)
        array = jnp.concatenate([before, array, after], axis=dim)
    return array


def cas_table(length):
    position = jnp.arange(length, dtype=jnp.int32)
    phase = position[:, None] * position[None, :] % length
    angle = 2.0 * jnp.pi / length * phase.astype(jnp.float32)
    return jnp.cos(angle) + jnp.sin(angle)


def transform_lateral(values):
    highest = lax.Precision.HIGHEST
    result = jnp.einsum("by,ayz->abz", cas_table(values.shape[1]), values, precision=highest)
    return jnp.einsum("cz,abz->abc", cas_table(values.shape[2]), result, precision=highest)


def plain_step(orbitals, energies, local_potential, lanczos, previous, beta):
    highest = lax.Precision.HIGHEST
    planes = lanczos.shape[1]
    length_y = lanczos.shape[2]
    length_z = lanczos.shape[3]
    length_x = planes * lax.axis_size("dom")
    normalizer = 4.0 * jnp.pi / (length_x * length_y * length_z)
    padded = extended(lanczos, (("dom", 1),), 3).astype(jnp.float32)
    current = padded[:, 3 : 3 + planes]
    laplace = 3.0 * central_weight * current
    for offset, weight in enumerate(side_weights):
        reach = offset + 1
        laplace = laplace + weight * (
            padded[:, 3 + reach : 3 + reach + planes] + padded[:, 3 - reach : 3 - reach + planes]
        )
        for dimension in (2, 3):
            laplace = laplace + weight * (
                jnp.roll(current, reach, dimension) + jnp.roll(current, -reach, dimension)
            )
    partial_density = jnp.sum(orbitals.astype(jnp.float32) * current, axis=0)
    square_x = wave_square(jnp.arange(length_x, dtype=jnp.int32), length_x)
    table_x = cas_table(length_x)
    density = lax.psum(partial_density.astype(jnp.bfloat16), "orb").astype(jnp.float32)
    spectrum = lax.all_to_all(
        transform_lateral(density), "dom", split_axis=1, concat_axis=0, tiled=True
    )
    row_count = spectrum.shape[1]
    index_y = lax.axis_index("dom") * row_count + jnp.arange(row_count, dtype=jnp.int32)
    square_y = wave_square(index_y, length_y)
    square_z = wave_square(jnp.arange(length_z, dtype=jnp.int32), length_z)
    summed = square_x[:, None, None] + square_y[None, :, None] + square_z[None, None, :] + screening
    spectrum = jnp.einsum("ax,xbc->abc", table_x, spectrum, precision=highest) * (
        normalizer / summed
    )
    spectrum = jnp.einsum("ax,xbc->abc", table_x, spectrum, precision=highest)
    spectrum = lax.all_to_all(
        spectrum.astype(jnp.bfloat16), "dom", split_axis=0, concat_axis=1, tiled=True
    ).astype(spectrum.dtype)
    potential = transform_lateral(spectrum)
    image = -0.5 * laplace + (local_potential[None] - energies[:, None, None, None]) * current
    image = image + orbitals.astype(jnp.float32) * potential[None]
    entries = float(lanczos.shape[0] * lax.axis_size("orb") * length_x * length_y * length_z)
    older = previous.astype(jnp.float32)
    beta_now = beta[0]
    moments = lax.psum(
        (
            jnp.sum(current * image),
            jnp.sum(image * image),
            jnp.sum(older * image),
            jnp.sum(current * current),
            jnp.sum(current * older),
            jnp.sum(older * older),
        ),
        ("dom", "orb"),
    )
    cross_mean = moments[0] / entries
    image_mean = moments[1] / entries
    older_image = moments[2] / entries
    self_mean = moments[3] / entries
    mixed_mean = moments[4] / entries
    older_mean = moments[5] / entries
    squares = image_mean - 2.0 * cross_mean * cross_mean - 2.0 * beta_now * older_image
    squares = (
        squares + cross_mean * cross_mean * self_mean + 2.0 * cross_mean * beta_now * mixed_mean
    )
    squares = squares + beta_now * beta_now * older_mean
    remainder = image - cross_mean * current - beta_now * older
    norm_next = jnp.sqrt(squares + 1e-06)
    next_vector = (remainder / norm_next).astype(jnp.bfloat16)
    return (next_vector, jnp.reshape(cross_mean, (1,)), jnp.reshape(norm_next, (1,)))


def per_device(orbitals, energies, local_potential, lanczos, previous, beta):
    _, planes, length_y, length_z = lanczos.shape
    groups = lax.axis_size("orb")
    devices = groups * lax.axis_size("dom")
    fits = planes % groups == 0 and planes >= reach_max
    fits = fits and length_y % (8 * devices) == 0 and length_z % 128 == 0
    step = split_step if fits else plain_step
    return step(orbitals, energies, local_potential, lanczos, previous, beta)


def solution(mesh):
    return jax.shard_map(
        per_device,
        mesh=mesh,
        in_specs=(
            P("orb", "dom", None, None),
            P("orb"),
            P("dom", None, None),
            P("orb", "dom", None, None),
            P("orb", "dom", None, None),
            P(),
        ),
        out_specs=(P("orb", "dom", None, None), P(), P()),
        check_vma=False,
    )
```
